32 devices in a mesh: gx: 4 (over x, core), gy: 8 (over z, y).
Axes of the slice: x: 2, y: 2, z: 4, core: 2. Of those that a mesh axis runs over, the one named last changes fastest.
Arguments:
- queries: bfloat16 [4, 8, 128, 768], P('gx', 'gy'), may hold values from -40 to 40
- keys_values: bfloat16 [4, 8, 2, 128, 768], P('gx', 'gy'), may hold values from -10 to 10
- out_grad: bfloat16 [4, 8, 128, 768], P('gx', 'gy'), may hold values from -6 to 6
- pattern: int32 [4, 8, 9], P('gx', 'gy'), may hold values 0 or 1
Outputs:
- attended: bfloat16 [4, 8, 128, 768], P('gx', 'gy')
- query_grad: bfloat16 [4, 8, 128, 768], P('gx', 'gy')
- key_value_grad: bfloat16 [4, 8, 2, 128, 768], P('gx', 'gy')
The draws below stay inside these ranges and needn't reach their ends.
All inputs are finite; a program needn't handle non-finite values. No bound on the sum of `pattern` on one device may be relied on, other than what follows from the above.
Results may differ from the reference program's by a relative error of at most 0.02.
Values may be sent and summed in bfloat16 or wider, within the bound.
No kernel may reach another device: no remote copies, remote signals or barrier semaphores. Data moves between devices by JAX's collectives and lax.ppermute only.
A program may use at most 128 MiB of HBM per device.

```python
import jax
import jax.numpy as jnp
from jax import lax

D = 768
H = 12
E = 64
BT = 128
LEVELS = 1
SLOTS = 9
BX = 4
BY = 8


def draw_common(key):
    base_key = jax.random.fold_in(key, 11)
    query_key, key_key, value_key = jax.random.split(base_key, 3)
    full_shape = (BX, BY, BT, D)
    query_rows = 1.6 * jax.random.truncated_normal(query_key, -6.0, 6.0, full_shape, jnp.float32)
    key_rows = 1.6 * jax.random.truncated_normal(key_key, -6.0, 6.0, full_shape, jnp.float32)
    value_rows = jax.random.truncated_normal(value_key, -6.0, 6.0, full_shape, jnp.float32)
    return (query_rows, jnp.stack([key_rows, value_rows], 2))


def draw_queries(key, part):
    return draw_common(key)[0].astype(jnp.bfloat16)


def draw_keys_values(key, part):
    return draw_common(key)[1].astype(jnp.bfloat16)


def with_ends(values, stream_key, least, top_value):
    shape = values.shape
    place = [jax.random.randint(jax.random.fold_in(stream_key, axis), (), 0, shape[axis]) for axis in range(len(shape))]
    values = values.at[tuple(place)].set(least)
    longest = shape.index(max(shape))
    place[longest] = (place[longest] + 1) % shape[longest]
    return values.at[tuple(place)].set(top_value)


def shard_levels(own_key, extent, pieces, low, high):
    def one(axis_at, shards_of):
        steps = jax.random.uniform(jax.random.fold_in(jax.random.fold_in(own_key, 6), axis_at), (shards_of,), jnp.float32, low / len(pieces), high / len(pieces))
        return jnp.repeat(jnp.exp(steps), extent[axis_at] // shards_of).reshape((-1,) + (1,) * (len(extent) - axis_at - 1))

    factor_of = one(*pieces[0])
    for cut in pieces[1:]:
        factor_of = factor_of * one(*cut)
    return factor_of


def centred(rng, extent, scale, limit, cuts=(), held_as=jnp.bfloat16):
    values = scale * jax.random.normal(rng, extent, jnp.float32)
    if cuts:
        values = values * shard_levels(rng, extent, cuts, -0.22, 0.18)
    return jnp.clip(values, -limit, limit).astype(held_as)


def setup_inputs(seed: int = 0) -> dict:
    keys = jax.random.split(jax.random.key(seed), 5)
    queries = draw_queries(jax.random.fold_in(keys[4], 71), 0)
    keys_values = draw_keys_values(jax.random.fold_in(keys[4], 71), 0)
    out_grad = centred(keys[2], (BX, BY, BT, D), 1.0, 6.0, ((0, 4), (1, 8)))
    pattern = with_ends((jax.random.randint(keys[3], (BX, BY, SLOTS), 0, 4) < 3).astype(jnp.int32), jax.random.fold_in(keys[3], 1), 0, 1)
    return {"queries": queries, "keys_values": keys_values, "out_grad": out_grad, "pattern": pattern}


def window_slot(position):
    return position if position < 4 else position - 1


def at(*starts):
    return tuple(jnp.asarray(s).astype(jnp.int32) for s in starts)


def block_pass(query_blk, grad_blk, blocks, usable, scaling):
    key_count = blocks.shape[0]
    key_rows = blocks[:, 0].reshape(key_count * BT, H, E).astype(jnp.float32)
    value_rows = blocks[:, 1].reshape(key_count * BT, H, E).astype(jnp.float32)
    query_part = query_blk.reshape(BT, H, E).astype(jnp.float32)
    upstream = grad_blk.reshape(BT, H, E).astype(jnp.float32)
    key_keep = jnp.repeat(usable, BT)
    scores = jnp.einsum("qhe,khe->hqk", query_part, key_rows) * scaling
    scores = jnp.where(key_keep[None, None, :], scores, jnp.float32(-jnp.inf))
    largest = jnp.max(scores, axis=-1, keepdims=True)
    raised = jnp.exp(scores - largest)
    totals = jnp.sum(raised, axis=-1, keepdims=True)
    weights = raised / totals
    weights_low = lax.optimization_barrier(weights.astype(jnp.bfloat16)).astype(jnp.float32)
    attended = jnp.einsum("hqk,khe->qhe", weights_low, value_rows).reshape(BT, D).astype(jnp.bfloat16)
    attended_wide = lax.optimization_barrier(attended).reshape(BT, H, E).astype(jnp.float32)
    row_delta = jnp.einsum("qhe,qhe->hq", upstream, attended_wide)
    prob_grad = jnp.einsum("qhe,khe->hqk", upstream, value_rows)
    score_grad = lax.optimization_barrier((weights * (prob_grad - row_delta[:, :, None])).astype(jnp.bfloat16)).astype(jnp.float32)
    query_grad = (jnp.einsum("hqk,khe->qhe", score_grad, key_rows) * scaling).reshape(BT, D).astype(jnp.bfloat16)
    key_grad = (jnp.einsum("hqk,qhe->khe", score_grad, query_part) * scaling).reshape(key_count, BT, D).astype(jnp.bfloat16)
    value_grad = jnp.einsum("hqk,qhe->khe", weights_low, upstream).reshape(key_count, BT, D).astype(jnp.bfloat16)
    return attended, query_grad, jnp.stack([key_grad, value_grad], 1)


def reference(queries, keys_values, out_grad, pattern):
    scaling = float(E) ** -0.5
    padded = jnp.pad(keys_values, ((1, 1), (1, 1), (0, 0), (0, 0), (0, 0)))

    def advance(totals, flat_index):
        block_x = (flat_index // BY).astype(jnp.int32)
        block_y = (flat_index % BY).astype(jnp.int32)
        query_blk = lax.dynamic_slice(queries, at(block_x, block_y, 0, 0), (1, 1, BT, D)).reshape(BT, D)
        grad_blk = lax.dynamic_slice(out_grad, at(block_x, block_y, 0, 0), (1, 1, BT, D)).reshape(BT, D)
        window = lax.dynamic_slice(padded, at(block_x, block_y, 0, 0, 0), (3, 3, 2, BT, D))
        partners = []
        for flip_bit in range(1, LEVELS + 1):
            partner_x = block_x ^ jnp.int32(1 << flip_bit)
            partners.append(lax.dynamic_slice(keys_values, at(partner_x, block_y, 0, 0, 0), (1, 1, 2, BT, D)).reshape(1, 2, BT, D))
        blocks = jnp.concatenate([window.reshape(9, 2, BT, D)] + partners)
        pattern_bits = lax.dynamic_slice(pattern, at(block_x, block_y, 0), (1, 1, SLOTS)).reshape(SLOTS) > 0
        usable = []
        for position in range(9):
            shift_x = position // 3 - 1
            shift_y = position % 3 - 1
            if position == 4:
                usable.append(jnp.array(True))
            else:
                inside = (block_x + shift_x >= 0) & (block_x + shift_x < BX) & (block_y + shift_y >= 0) & (block_y + shift_y < BY)
                usable.append(inside & pattern_bits[window_slot(position)])
        for flip_bit in range(1, LEVELS + 1):
            usable.append(pattern_bits[7 + flip_bit])
        attended, query_grad, pair_grads = block_pass(query_blk, grad_blk, blocks, jnp.stack(usable), scaling)
        existing = lax.dynamic_slice(totals, at(block_x, block_y, 0, 0, 0), (3, 3, 2, BT, D))
        totals = lax.dynamic_update_slice(totals, existing + pair_grads[:9].reshape(3, 3, 2, BT, D).astype(jnp.float32), at(block_x, block_y, 0, 0, 0))
        for flip_bit in range(1, LEVELS + 1):
            location = at((block_x ^ jnp.int32(1 << flip_bit)) + 1, block_y + 1, 0, 0, 0)
            existing = lax.dynamic_slice(totals, location, (1, 1, 2, BT, D))
            totals = lax.dynamic_update_slice(totals, existing + pair_grads[8 + flip_bit].reshape(1, 1, 2, BT, D).astype(jnp.float32), location)
        return totals, (attended, query_grad)

    initial = jnp.zeros((BX + 2, BY + 2, 2, BT, D), jnp.float32)
    totals, (attended, query_grad) = lax.scan(advance, initial, jnp.arange(BX * BY, dtype=jnp.int32))
    return (attended.reshape(BX, BY, BT, D), query_grad.reshape(BX, BY, BT, D), totals[1:-1, 1:-1].astype(jnp.bfloat16))
```

```python
import functools
import math

import jax
import jax.numpy as jnp
from jax import lax
from jax.experimental import pallas as pl
from jax.experimental.pallas import tpu as pltpu
from jax.sharding import PartitionSpec as P

E = 64
LANES = 128
PENALTY = 1e30
FOLD = math.log2(math.e) * float(E) ** (-0.5)
SCALE = float(E) ** (-0.5)
CONTRACT_LAST = (((1,), (1,)), ((), ()))


def pair_swap(value, axis, offset):
    pairs = []
    for first in range(offset, lax.axis_size(axis) - 1, 2):
        pairs += [(first, first + 1), (first + 1, first)]
    return lax.ppermute(value, axis, pairs)


def partner_swap(value, level):
    return lax.ppermute(value, "gx", [(i, i ^ (1 << level)) for i in range(lax.axis_size("gx"))])


def split_heads(block):
    low = lax.broadcasted_iota(jnp.int32, block.shape, 1) < E
    zero = jnp.zeros_like(block)
    return jnp.concatenate([jnp.where(low, block, zero), jnp.where(low, zero, block)], axis=0)


def join_heads(stacked):
    rows = stacked.shape[0] // 2
    low = lax.broadcasted_iota(jnp.int32, (rows, LANES), 1) < E
    return jnp.where(low, stacked[:rows], stacked[rows:])


def query_kernel(count, bias_ref, q_ref, do_ref, flags_ref, *refs):
    kv_refs = refs[:count]
    att_ref, dq_ref, stats_ref = refs[count:]
    rows, width = q_ref.shape
    heads = width // E
    lane = lax.broadcasted_iota(jnp.int32, (rows, LANES), 1)
    low = lane < E
    stats = jnp.zeros((rows, LANES), jnp.float32)
    for pair in range(width // LANES):
        cols = slice(pair * LANES, (pair + 1) * LANES)
        grad = do_ref[:, cols]
        keys = jnp.concatenate([r[0, :, cols] for r in kv_refs], axis=0)
        values = jnp.concatenate([r[1, :, cols] for r in kv_refs], axis=0)
        scores = lax.dot_general(
            split_heads(q_ref[:, cols]), keys, CONTRACT_LAST, preferred_element_type=jnp.float32
        )
        scores = jnp.concatenate(
            [scores[:, b * rows : (b + 1) * rows] + bias_ref[b] for b in range(count)], axis=1
        )
        largest = jnp.max(scores, axis=1, keepdims=True) * FOLD
        raised = jnp.exp2(scores * FOLD - largest)
        totals = jnp.sum(raised, axis=1, keepdims=True)
        inverse = 1.0 / totals
        attended = jnp.dot(
            raised.astype(jnp.bfloat16), values, preferred_element_type=jnp.float32
        )
        attended = join_heads(attended * inverse).astype(jnp.bfloat16)
        att_ref[:, cols] = attended
        product = grad.astype(jnp.float32) * attended.astype(jnp.float32)
        delta = jnp.concatenate(
            [
                jnp.sum(jnp.where(low, product, 0.0), axis=1, keepdims=True),
                jnp.sum(jnp.where(low, 0.0, product), axis=1, keepdims=True),
            ],
            axis=0,
        )
        prob_grad = lax.dot_general(
            split_heads(grad), values, CONTRACT_LAST, preferred_element_type=jnp.float32
        )
        score_grad = (raised * (prob_grad - delta)).astype(jnp.bfloat16)
        query_grad = jnp.dot(score_grad, keys, preferred_element_type=jnp.float32)
        dq_ref[:, cols] = join_heads(query_grad * (inverse * SCALE)).astype(jnp.bfloat16)
        level = largest + jnp.log2(totals)
        for half in range(2):
            head = 2 * pair + half
            part = slice(half * rows, (half + 1) * rows)
            stats = jnp.where(lane == head, level[part], stats)
            stats = jnp.where(lane == heads + head, delta[part], stats)
    turned = stats.T
    stats_ref[: 2 * heads] = turned[: 2 * heads]
    stats_ref[2 * heads :] = flags_ref[...]


def key_kernel(count, slots, index_ref, choose_ref, kv_ref, q_ref, do_ref, *refs):
    qd_refs = refs[: count - 1]
    stat_refs = refs[count - 1 : count + 2]
    out_ref = refs[count + 2]
    rows, width = q_ref.shape
    heads = width // E
    levels, deltas = [], []
    for b in range(count):
        stat = stat_refs[slots[b]][index_ref[b]]
        flag = jnp.sum(
            stat[2 * heads : 2 * heads + 1] * choose_ref[b : b + 1], axis=1, keepdims=True
        )
        levels.append(stat[:heads] + jnp.where(flag > 0.5, 0.0, PENALTY))
        deltas.append(stat[heads : 2 * heads])
    levels = jnp.concatenate(levels, axis=1)
    deltas = jnp.concatenate(deltas, axis=1)

    def per_head(table, pair):
        shape = (rows, table.shape[1])
        return jnp.concatenate(
            [jnp.broadcast_to(table[2 * pair + h : 2 * pair + h + 1], shape) for h in range(2)],
            axis=0,
        )

    for pair in range(width // LANES):
        cols = slice(pair * LANES, (pair + 1) * LANES)
        queries = jnp.concatenate([q_ref[:, cols]] + [r[0, :, cols] for r in qd_refs], axis=0)
        grads = jnp.concatenate([do_ref[:, cols]] + [r[1, :, cols] for r in qd_refs], axis=0)
        scores = lax.dot_general(
            split_heads(kv_ref[0, :, cols]),
            queries,
            CONTRACT_LAST,
            preferred_element_type=jnp.float32,
        )
        weights = jnp.exp2(scores * FOLD - per_head(levels, pair))
        value_grad = jnp.dot(
            weights.astype(jnp.bfloat16), grads, preferred_element_type=jnp.float32
        )
        prob_grad = lax.dot_general(
            split_heads(kv_ref[1, :, cols]),
            grads,
            CONTRACT_LAST,
            preferred_element_type=jnp.float32,
        )
        score_grad = (weights * (prob_grad - per_head(deltas, pair))).astype(jnp.bfloat16)
        key_grad = jnp.dot(score_grad, queries, preferred_element_type=jnp.float32)
        out_ref[0, :, cols] = (join_heads(key_grad) * SCALE).astype(jnp.bfloat16)
        out_ref[1, :, cols] = join_heads(value_grad).astype(jnp.bfloat16)


VMEM = pl.BlockSpec(memory_space=pltpu.VMEM)
SMEM = pl.BlockSpec(memory_space=pltpu.SMEM)


def cost(rows, width, count):
    return pl.CostEstimate(
        flops=8 * rows * rows * width * count,
        bytes_accessed=4 * rows * width * (count + 3),
        transcendentals=rows * rows * (width // E) * count,
    )


def per_device(queries, keys_values, out_grad, pattern):
    own_q, own_kv, own_do = queries[0, 0], keys_values[0, 0], out_grad[0, 0]
    rows, width = own_q.shape
    heads = width // E
    columns, lines = lax.axis_size("gx"), lax.axis_size("gy")
    levels = columns.bit_length() - 2
    column, line = lax.axis_index("gx"), lax.axis_index("gy")
    side = 1 - 2 * (column % 2)
    turn = 1 - 2 * (line % 2)

    def exchange_row(value):
        pair = pair_swap(value, "gx", 0)
        partners = [partner_swap(value, level) for level in range(1, levels + 1)]
        if columns == 4:
            other = pair_swap(partners[0], "gx", 0)
        else:
            other = pair_swap(value, "gx", 1)
        return [pair, other] + partners

    def exchange_lines(value):
        return pair_swap(value, "gy", 1), pair_swap(value, "gy", 0)

    def spread(value):
        return [value, pair_swap(value, "gx", 0), pair_swap(value, "gx", 1)]

    far_kv, near_kv = exchange_lines(own_kv)
    row_kv = exchange_row(own_kv)
    own_qd = jnp.stack([own_q, own_do])
    far_qd, near_qd = exchange_lines(own_qd)
    row_qd = exchange_row(own_qd)
    kv_blocks = [own_kv] + row_kv + spread(far_kv) + spread(near_kv)

    shift_x = [0, side, -side] + [0] * levels + [0, side, -side] * 2
    shift_y = [0] * (3 + levels) + [-turn] * 3 + [turn] * 3
    count = len(kv_blocks)
    slots = [0] * (3 + levels) + [1] * 3 + [2] * 3
    shift_x = jnp.stack([jnp.asarray(v, jnp.int32) for v in shift_x])
    shift_y = jnp.stack([jnp.asarray(v, jnp.int32) for v in shift_y])
    position = jnp.arange(count)
    level = position - 2
    is_partner = (level >= 1) & (level <= levels)
    place = (shift_x + 1) * 3 + shift_y + 1
    flag = jnp.where(is_partner, 7 + level, jnp.where(place < 4, place, place - 1))
    mirrored = jnp.where(is_partner, 7 + level, 7 - flag)
    target_x = jnp.where(is_partner, column ^ (1 << jnp.maximum(level, 0)), column + shift_x)
    target_y = line + shift_y
    inside = (target_x >= 0) & (target_x < columns) & (target_y >= 0) & (target_y < lines)
    is_own = position == 0
    bits = pattern[0, 0]
    kinds = jnp.arange(bits.shape[0])
    chosen = jnp.sum(jnp.where(flag[:, None] == kinds[None], bits[None], 0), axis=1) > 0
    bias = jnp.where(is_own | (inside & chosen), 0.0, -PENALTY).astype(jnp.float32)
    index = jnp.clip(target_x, 0, columns - 1).astype(jnp.int32)
    lanes = jnp.arange(LANES)
    wanted = jnp.where(is_own, LANES - 1, jnp.where(inside, mirrored, -1))
    choose = (wanted[:, None] == lanes[None]).astype(jnp.float32)
    flags = jnp.pad((bits > 0).astype(jnp.float32), (0, LANES - bits.shape[0]))
    flags = jnp.where(lanes == LANES - 1, 1.0, flags)
    flags = jnp.broadcast_to(flags[None], (8, LANES))

    attended, query_grad, stats = pl.pallas_call(
        functools.partial(query_kernel, count),
        out_shape=(
            jax.ShapeDtypeStruct((rows, width), jnp.bfloat16),
            jax.ShapeDtypeStruct((rows, width), jnp.bfloat16),
            jax.ShapeDtypeStruct((2 * heads + 8, LANES), jnp.float32),
        ),
        in_specs=[SMEM] + [VMEM] * (3 + count),
        out_specs=(VMEM, VMEM, VMEM),
        cost_estimate=cost(rows, width, count),
    )(bias, own_q, own_do, flags, *kv_blocks)

    row_stats = lax.all_gather(stats, "gx")
    far_stats, near_stats = exchange_lines(row_stats)
    qd_blocks = row_qd + spread(far_qd) + spread(near_qd)
    key_value_grad = pl.pallas_call(
        functools.partial(key_kernel, count, slots),
        out_shape=jax.ShapeDtypeStruct(own_kv.shape, jnp.bfloat16),
        in_specs=[SMEM] + [VMEM] * (4 + count - 1 + 3),
        out_specs=VMEM,
        cost_estimate=cost(rows, width, count),
    )(index, choose, own_kv, own_q, own_do, *qd_blocks, row_stats, far_stats, near_stats)
    return attended[None, None], query_grad[None, None], key_value_grad[None, None]


def solution(mesh):
    placed = (
        P("gx", "gy", None, None),
        P("gx", "gy", None, None, None),
        P("gx", "gy", None, None),
        P("gx", "gy", None),
    )
    return jax.shard_map(
        per_device,
        mesh=mesh,
        in_specs=placed,
        out_specs=(
            P("gx", "gy", None, None),
            P("gx", "gy", None, None),
            P("gx", "gy", None, None, None),
        ),
        check_vma=False,
    )
```

```python
import functools
import math

import jax
import jax.numpy as jnp
from jax import lax
from jax.experimental import pallas as pl
from jax.experimental.pallas import tpu as pltpu
from jax.sharding import PartitionSpec as P

E = 64
LANES = 128
PENALTY = 1e30
FOLD = math.log2(math.e) * float(E) ** (-0.5)
SCALE = float(E) ** (-0.5)
CONTRACT_LAST = (((1,), (1,)), ((), ()))


def pair_swap(value, axis, offset):
    pairs = []
    for first in range(offset, lax.axis_size(axis) - 1, 2):
        pairs += [(first, first + 1), (first + 1, first)]
    return lax.ppermute(value, axis, pairs)


def partner_swap(value, level):
    return lax.ppermute(value, "gx", [(i, i ^ (1 << level)) for i in range(lax.axis_size("gx"))])


def split_heads(block):
    low = lax.broadcasted_iota(jnp.int32, block.shape, 1) < E
    zero = jnp.zeros_like(block)
    return jnp.concatenate([jnp.where(low, block, zero), jnp.where(low, zero, block)], axis=0)


def join_heads(stacked):
    rows = stacked.shape[0] // 2
    low = lax.broadcasted_iota(jnp.int32, (rows, LANES), 1) < E
    return jnp.where(low, stacked[:rows], stacked[rows:])


def query_kernel(count, first, last, bias_ref, q_ref, do_ref, flags_ref, *refs):
    kv_refs, refs = refs[:count], refs[count:]
    carried, (att_ref, dq_ref, stats_ref) = refs[:-3], refs[-3:]
    rows, width = q_ref.shape
    heads = width // E
    lane = lax.broadcasted_iota(jnp.int32, (rows, LANES), 1)
    low = lane < E
    stats = jnp.zeros((rows, LANES), jnp.float32)
    for pair in range(first, last):
        cols = slice(pair * LANES, (pair + 1) * LANES)
        out_cols = cols if last * LANES == width else slice((pair - first) * LANES, (pair - first + 1) * LANES)
        grad = do_ref[:, cols]
        keys = jnp.concatenate([r[0, :, cols] for r in kv_refs], axis=0)
        values = jnp.concatenate([r[1, :, cols] for r in kv_refs], axis=0)
        scores = lax.dot_general(
            split_heads(q_ref[:, cols]), keys, CONTRACT_LAST, preferred_element_type=jnp.float32
        )
        scores = jnp.concatenate(
            [scores[:, b * rows : (b + 1) * rows] + bias_ref[b] for b in range(count)], axis=1
        )
        largest = jnp.max(scores, axis=1, keepdims=True) * FOLD
        raised = jnp.exp2(scores * FOLD - largest)
        totals = jnp.sum(raised, axis=1, keepdims=True)
        inverse = 1.0 / totals
        attended = jnp.dot(
            raised.astype(jnp.bfloat16), values, preferred_element_type=jnp.float32
        )
        attended = join_heads(attended * inverse).astype(jnp.bfloat16)
        att_ref[:, out_cols] = attended
        product = grad.astype(jnp.float32) * attended.astype(jnp.float32)
        delta = jnp.concatenate(
            [
                jnp.sum(jnp.where(low, product, 0.0), axis=1, keepdims=True),
                jnp.sum(jnp.where(low, 0.0, product), axis=1, keepdims=True),
            ],
            axis=0,
        )
        prob_grad = lax.dot_general(
            split_heads(grad), values, CONTRACT_LAST, preferred_element_type=jnp.float32
        )
        score_grad = (raised * (prob_grad - delta)).astype(jnp.bfloat16)
        query_grad = jnp.dot(score_grad, keys, preferred_element_type=jnp.float32)
        dq_ref[:, out_cols] = join_heads(query_grad * (inverse * SCALE)).astype(jnp.bfloat16)
        level = largest + jnp.log2(totals)
        for half in range(2):
            head = 2 * pair + half
            part = slice(half * rows, (half + 1) * rows)
            stats = jnp.where(lane == head, level[part], stats)
            stats = jnp.where(lane == heads + head, delta[part], stats)
    turned = stats.T[: 2 * heads]
    if carried:
        att_in, dq_in, stats_in = carried
        done = first * LANES
        att_ref[:, :done] = att_in[...]
        dq_ref[:, :done] = dq_in[...]
        turned = turned + stats_in[: 2 * heads]
    stats_ref[: 2 * heads] = turned
    stats_ref[2 * heads :] = flags_ref[...]


def key_kernel(count, slots, bases, index_ref, choose_ref, kv_ref, q_ref, do_ref, *refs):
    qd_refs = refs[: count - 1]
    stat_refs = refs[count - 1 : count + 2]
    out_ref = refs[count + 2]
    rows, width = q_ref.shape
    heads = width // E
    levels, deltas = [], []
    for b in range(count):
        stat = stat_refs[slots[b]][index_ref[b]]
        flag = jnp.sum(
            stat[2 * heads : 2 * heads + 1] * choose_ref[b : b + 1], axis=1, keepdims=True
        )
        levels.append(stat[:heads] + jnp.where(flag > 0.5, 0.0, PENALTY))
        deltas.append(stat[heads : 2 * heads])
    levels = jnp.concatenate(levels, axis=1)
    deltas = jnp.concatenate(deltas, axis=1)

    def per_head(table, pair):
        shape = (rows, table.shape[1])
        return jnp.concatenate(
            [jnp.broadcast_to(table[2 * pair + h : 2 * pair + h + 1], shape) for h in range(2)],
            axis=0,
        )

    for pair in range(width // LANES):
        cols = slice(pair * LANES, (pair + 1) * LANES)
        queries = jnp.concatenate([q_ref[:, cols]] + [r[o, :, cols] for r, o in zip(qd_refs, bases)], axis=0)
        grads = jnp.concatenate([do_ref[:, cols]] + [r[o + 1, :, cols] for r, o in zip(qd_refs, bases)], axis=0)
        scores = lax.dot_general(
            split_heads(kv_ref[0, :, cols]),
            queries,
            CONTRACT_LAST,
            preferred_element_type=jnp.float32,
        )
        weights = jnp.exp2(scores * FOLD - per_head(levels, pair))
        value_grad = jnp.dot(
            weights.astype(jnp.bfloat16), grads, preferred_element_type=jnp.float32
        )
        prob_grad = lax.dot_general(
            split_heads(kv_ref[1, :, cols]),
            grads,
            CONTRACT_LAST,
            preferred_element_type=jnp.float32,
        )
        score_grad = (weights * (prob_grad - per_head(deltas, pair))).astype(jnp.bfloat16)
        key_grad = jnp.dot(score_grad, queries, preferred_element_type=jnp.float32)
        out_ref[0, :, cols] = (join_heads(key_grad) * SCALE).astype(jnp.bfloat16)
        out_ref[1, :, cols] = join_heads(value_grad).astype(jnp.bfloat16)


def after(value, other):
    return lax.optimization_barrier((value, other))[0]


def both(a, b):
    return lax.optimization_barrier((a, b))


def on_chip(value):
    return pltpu.with_memory_space_constraint(value, pltpu.MemorySpace.VMEM)


PARAMS = pltpu.CompilerParams(vmem_limit_bytes=24 * 2**20)
VMEM = pl.BlockSpec(memory_space=pltpu.VMEM)
SMEM = pl.BlockSpec(memory_space=pltpu.SMEM)


def cost(rows, width, count):
    return pl.CostEstimate(
        flops=64 * rows * rows * width * count,
        bytes_accessed=4 * rows * width * (count + 3),
        transcendentals=rows * rows * (width // E) * count,
    )


def per_device(queries, keys_values, out_grad, pattern):
    own_q, own_kv, own_do = queries[0, 0], keys_values[0, 0], out_grad[0, 0]
    rows, width = own_q.shape
    heads = width // E
    columns, lines = lax.axis_size("gx"), lax.axis_size("gy")
    levels = columns.bit_length() - 2
    column, line = lax.axis_index("gx"), lax.axis_index("gy")
    side = 1 - 2 * (column % 2)
    turn = 1 - 2 * (line % 2)

    def core_pair(value, tag):
        with jax.named_scope(tag + "_X1"):
            return pair_swap(value, "gx", 0)

    def link_pair(value, tag):
        with jax.named_scope(tag + "_X2"):
            return pair_swap(value, "gx", 1)

    def far(value, tag):
        with jax.named_scope(tag + "_far"):
            return pair_swap(value, "gy", 1)

    def near(value, tag):
        with jax.named_scope(tag + "_near"):
            return pair_swap(value, "gy", 0)

    def partners_of(value, tag):
        with jax.named_scope(tag + "_PT"):
            return [partner_swap(value, level) for level in range(1, levels + 1)]

    def other_side(value, partners, tag):
        if columns == 4:
            return core_pair(partners[0], tag + "_PT")
        return link_pair(value, tag)

    kv_far = far(own_kv, "kv")
    kv_near = near(own_kv, "kv")
    kv_pair = core_pair(own_kv, "kv")
    kv_partners = partners_of(after(own_kv, kv_pair), "kv")
    ready = after(kv_far, kv_pair)
    kv_far1, kv_far2 = core_pair(ready, "kvfar"), link_pair(ready, "kvfar")
    kv_other = other_side(own_kv, kv_partners, "kv")
    ready = after(kv_near, (kv_far1, kv_far2, kv_other))
    kv_near1, kv_near2 = core_pair(ready, "kvnear"), link_pair(ready, "kvnear")
    own_qd = jnp.stack([after(own_q, kv_far), own_do])
    ready = after(own_qd, (kv_near, kv_far1, kv_far2, kv_other))
    qd_far, qd_near = far(ready, "qd"), near(ready, "qd")
    ready = after(own_qd, kv_near1)
    qd_pair, qd_partners = core_pair(ready, "qd"), partners_of(ready, "qd")
    kv_blocks = [own_kv, kv_pair, kv_other] + kv_partners
    kv_blocks += [kv_far, kv_far1, kv_far2, kv_near, kv_near1, kv_near2]
    kv_blocks = [on_chip(block) for block in kv_blocks]

    shift_x = [0, side, -side] + [0] * levels + [0, side, -side] * 2
    shift_y = [0] * (3 + levels) + [-turn] * 3 + [turn] * 3
    count = len(kv_blocks)
    slots = [0] * (3 + levels) + [1] * 3 + [2] * 3
    shift_x = jnp.stack([jnp.asarray(v, jnp.int32) for v in shift_x])
    shift_y = jnp.stack([jnp.asarray(v, jnp.int32) for v in shift_y])
    position = jnp.arange(count)
    level = position - 2
    is_partner = (level >= 1) & (level <= levels)
    place = (shift_x + 1) * 3 + shift_y + 1
    flag = jnp.where(is_partner, 7 + level, jnp.where(place < 4, place, place - 1))
    mirrored = jnp.where(is_partner, 7 + level, 7 - flag)
    target_x = jnp.where(is_partner, column ^ (1 << jnp.maximum(level, 0)), column + shift_x)
    target_y = line + shift_y
    inside = (target_x >= 0) & (target_x < columns) & (target_y >= 0) & (target_y < lines)
    is_own = position == 0
    bits = pattern[0, 0]
    kinds = jnp.arange(bits.shape[0])
    chosen = jnp.sum(jnp.where(flag[:, None] == kinds[None], bits[None], 0), axis=1) > 0
    bias = jnp.where(is_own | (inside & chosen), 0.0, -PENALTY).astype(jnp.float32)
    index = jnp.clip(target_x, 0, columns - 1).astype(jnp.int32)
    lanes = jnp.arange(LANES)
    wanted = jnp.where(is_own, LANES - 1, jnp.where(inside, mirrored, -1))
    choose = (wanted[:, None] == lanes[None]).astype(jnp.float32)
    flags = jnp.pad((bits > 0).astype(jnp.float32), (0, LANES - bits.shape[0]))
    flags = jnp.where(lanes == LANES - 1, 1.0, flags)
    flags = jnp.broadcast_to(flags[None], (8, LANES))

    def query_side(first, last, carried):
        full = last * LANES == width
        part = jax.ShapeDtypeStruct(
            (rows, width if full else (last - first) * LANES), jnp.bfloat16
        )
        return pl.pallas_call(
            functools.partial(query_kernel, count, first, last),
            out_shape=(
                part,
                part,
                jax.ShapeDtypeStruct((2 * heads + 8, LANES), jnp.float32),
            ),
            in_specs=[SMEM] + [VMEM] * (3 + count + len(carried)),
            out_specs=(VMEM, VMEM, VMEM),
            compiler_params=PARAMS,
            cost_estimate=cost(rows, (last - first) * LANES, count),
        )(bias, own_q, own_do, flags, *kv_blocks, *carried)

    attended, query_grad, stats = query_side(0, width // LANES, ())
    stats, qd_far, qd_partners = lax.optimization_barrier((stats, qd_far, qd_partners))
    qd_far1, qd_far2 = core_pair(qd_far, "qdfar"), link_pair(qd_far, "qdfar")
    qd_other = other_side(own_qd, qd_partners, "qd")
    with jax.named_scope("stats_row"):
        row_stats = lax.all_gather(after(stats, (qd_far1, qd_other, qd_pair)), "gx")
    ready = after(qd_near, row_stats)
    qd_near1, qd_near2 = core_pair(ready, "qdnear"), link_pair(ready, "qdnear")
    far_stats, near_stats = far(row_stats, "stats"), near(row_stats, "stats")
    qd_blocks = [qd_pair, qd_other] + qd_partners
    qd_blocks += [qd_far, qd_far1, qd_far2, qd_near, qd_near1, qd_near2]
    qd_blocks = [on_chip(block) for block in qd_blocks]
    bases = [0] * len(qd_blocks)
    key_value_grad = pl.pallas_call(
        functools.partial(key_kernel, count, slots, bases),
        out_shape=jax.ShapeDtypeStruct(own_kv.shape, jnp.bfloat16),
        in_specs=[SMEM] + [VMEM] * (4 + count - 1 + 3),
        out_specs=VMEM,
        compiler_params=PARAMS,
        cost_estimate=cost(rows, width, count),
    )(index, choose, own_kv, own_q, own_do, *qd_blocks, row_stats, far_stats, near_stats)
    return attended[None, None], query_grad[None, None], key_value_grad[None, None]


def solution(mesh):
    placed = (
        P("gx", "gy", None, None),
        P("gx", "gy", None, None, None),
        P("gx", "gy", None, None),
        P("gx", "gy", None),
    )
    return jax.shard_map(
        per_device,
        mesh=mesh,
        in_specs=placed,
        out_specs=(
            P("gx", "gy", None, None),
            P("gx", "gy", None, None),
            P("gx", "gy", None, None, None),
        ),
        check_vma=False,
    )
```

```python
import functools
import math

import jax
import jax.numpy as jnp
from jax import lax
from jax.experimental import pallas as pl
from jax.experimental.pallas import tpu as pltpu
from jax.sharding import PartitionSpec as P

E = 64
LANES = 128
PENALTY = 1e30
FOLD = math.log2(math.e) * float(E) ** (-0.5)
SCALE = float(E) ** (-0.5)
CONTRACT_LAST = (((1,), (1,)), ((), ()))


def pair_swap(value, axis, offset):
    pairs = []
    for first in range(offset, lax.axis_size(axis) - 1, 2):
        pairs += [(first, first + 1), (first + 1, first)]
    return lax.ppermute(value, axis, pairs)


def partner_swap(value, level):
    return lax.ppermute(value, "gx", [(i, i ^ (1 << level)) for i in range(lax.axis_size("gx"))])


def split_heads(block):
    low = lax.broadcasted_iota(jnp.int32, block.shape, 1) < E
    zero = jnp.zeros_like(block)
    return jnp.concatenate([jnp.where(low, block, zero), jnp.where(low, zero, block)], axis=0)


def join_heads(stacked):
    rows = stacked.shape[0] // 2
    low = lax.broadcasted_iota(jnp.int32, (rows, LANES), 1) < E
    return jnp.where(low, stacked[:rows], stacked[rows:])


def per_lane(columns, lane, first, table):
    rows = table.shape[0]
    table = jnp.where(lane == first, columns[:rows], table)
    return jnp.where(lane == first + 1, columns[rows:], table)


def from_lanes(table, first):
    return jnp.concatenate([table[:, first : first + 1], table[:, first + 1 : first + 2]], axis=0)


def masked_scores(q_ref, kv_refs, bias_ref, start, cols):
    rows = q_ref.shape[0]
    keys = jnp.concatenate([r[0, :, cols] for r in kv_refs], axis=0)
    scores = lax.dot_general(
        split_heads(q_ref[:, cols]), keys, CONTRACT_LAST, preferred_element_type=jnp.float32
    )
    return keys, [
        scores[:, b * rows : (b + 1) * rows] + bias_ref[start + b] for b in range(len(kv_refs))
    ]


def attend_kernel(count, bias_ref, q_ref, do_ref, flags_ref, *refs):
    kv_refs, (att_ref, columns_ref, stats_ref) = refs[:count], refs[count:]
    rows, width = q_ref.shape
    heads = width // E
    lane = lax.broadcasted_iota(jnp.int32, (rows, LANES), 1)
    low = lane < E
    columns = jnp.zeros((rows, LANES), jnp.float32)
    for pair in range(width // LANES):
        cols = slice(pair * LANES, (pair + 1) * LANES)
        values = jnp.concatenate([r[1, :, cols] for r in kv_refs], axis=0)
        _, scores = masked_scores(q_ref, kv_refs, bias_ref, 0, cols)
        scores = jnp.concatenate(scores, axis=1)
        largest = jnp.max(scores, axis=1, keepdims=True) * FOLD
        raised = jnp.exp2(scores * FOLD - largest)
        totals = jnp.sum(raised, axis=1, keepdims=True)
        sums = jnp.dot(raised.astype(jnp.bfloat16), values, preferred_element_type=jnp.float32)
        attended = join_heads(sums * (1.0 / totals)).astype(jnp.bfloat16)
        att_ref[:, cols] = attended
        product = do_ref[:, cols].astype(jnp.float32) * attended.astype(jnp.float32)
        delta = jnp.concatenate(
            [
                jnp.sum(jnp.where(low, product, 0.0), axis=1, keepdims=True),
                jnp.sum(jnp.where(low, 0.0, product), axis=1, keepdims=True),
            ],
            axis=0,
        )
        columns = per_lane(largest + jnp.log2(totals), lane, 2 * pair, columns)
        columns = per_lane(delta, lane, heads + 2 * pair, columns)
    columns_ref[...] = columns
    stats_ref[: 2 * heads] = columns.T[: 2 * heads]
    stats_ref[2 * heads :] = flags_ref[...]


def query_kernel(count, bias_ref, q_ref, do_ref, columns_ref, *refs):
    kv_refs, dq_ref = refs[:count], refs[count]
    rows, width = q_ref.shape
    heads = width // E
    columns = columns_ref[...]
    for pair in range(width // LANES):
        cols = slice(pair * LANES, (pair + 1) * LANES)
        values = jnp.concatenate([r[1, :, cols] for r in kv_refs], axis=0)
        keys, scores = masked_scores(q_ref, kv_refs, bias_ref, 0, cols)
        weights = jnp.exp2(
            jnp.concatenate(scores, axis=1) * FOLD - from_lanes(columns, 2 * pair)
        )
        prob_grad = lax.dot_general(
            split_heads(do_ref[:, cols]), values, CONTRACT_LAST, preferred_element_type=jnp.float32
        )
        delta = from_lanes(columns, heads + 2 * pair)
        score_grad = (weights * (prob_grad - delta)).astype(jnp.bfloat16)
        query_grad = jnp.dot(score_grad, keys, preferred_element_type=jnp.float32)
        dq_ref[:, cols] = (join_heads(query_grad) * SCALE).astype(jnp.bfloat16)


def key_kernel(count, slots, bases, index_ref, choose_ref, kv_ref, q_ref, do_ref, *refs):
    qd_refs = refs[: count - 1]
    stat_refs = refs[count - 1 : count + 2]
    out_ref = refs[count + 2]
    rows, width = q_ref.shape
    heads = width // E
    levels, deltas = [], []
    for b in range(count):
        stat = stat_refs[slots[b]][index_ref[b]]
        flag = jnp.sum(
            stat[2 * heads : 2 * heads + 1] * choose_ref[b : b + 1], axis=1, keepdims=True
        )
        levels.append(stat[:heads] + jnp.where(flag > 0.5, 0.0, PENALTY))
        deltas.append(stat[heads : 2 * heads])
    levels = jnp.concatenate(levels, axis=1)
    deltas = jnp.concatenate(deltas, axis=1)

    def per_head(table, pair):
        shape = (rows, table.shape[1])
        return jnp.concatenate(
            [jnp.broadcast_to(table[2 * pair + h : 2 * pair + h + 1], shape) for h in range(2)],
            axis=0,
        )

    for pair in range(width // LANES):
        cols = slice(pair * LANES, (pair + 1) * LANES)
        queries = jnp.concatenate([q_ref[:, cols]] + [r[o, :, cols] for r, o in zip(qd_refs, bases)], axis=0)
        grads = jnp.concatenate([do_ref[:, cols]] + [r[o + 1, :, cols] for r, o in zip(qd_refs, bases)], axis=0)
        scores = lax.dot_general(
            split_heads(kv_ref[0, :, cols]),
            queries,
            CONTRACT_LAST,
            preferred_element_type=jnp.float32,
        )
        weights = jnp.exp2(scores * FOLD - per_head(levels, pair))
        value_grad = jnp.dot(
            weights.astype(jnp.bfloat16), grads, preferred_element_type=jnp.float32
        )
        prob_grad = lax.dot_general(
            split_heads(kv_ref[1, :, cols]),
            grads,
            CONTRACT_LAST,
            preferred_element_type=jnp.float32,
        )
        score_grad = (weights * (prob_grad - per_head(deltas, pair))).astype(jnp.bfloat16)
        key_grad = jnp.dot(score_grad, queries, preferred_element_type=jnp.float32)
        out_ref[0, :, cols] = (join_heads(key_grad) * SCALE).astype(jnp.bfloat16)
        out_ref[1, :, cols] = join_heads(value_grad).astype(jnp.bfloat16)


def after(value, other):
    return lax.optimization_barrier((value, other))[0]


def both(a, b):
    return lax.optimization_barrier((a, b))


def on_chip(value):
    return pltpu.with_memory_space_constraint(value, pltpu.MemorySpace.VMEM)


PARAMS = pltpu.CompilerParams(vmem_limit_bytes=14 * 2**20)
VMEM = pl.BlockSpec(memory_space=pltpu.VMEM)
SMEM = pl.BlockSpec(memory_space=pltpu.SMEM)


COST = pl.CostEstimate(flops=128, bytes_accessed=128, transcendentals=0)


def per_device(queries, keys_values, out_grad, pattern):
    own_q, own_kv, own_do = queries[0, 0], keys_values[0, 0], out_grad[0, 0]
    rows, width = own_q.shape
    heads = width // E
    columns, lines = lax.axis_size("gx"), lax.axis_size("gy")
    levels = columns.bit_length() - 2
    column, line = lax.axis_index("gx"), lax.axis_index("gy")
    side = 1 - 2 * (column % 2)
    turn = 1 - 2 * (line % 2)

    def core_pair(value, tag):
        with jax.named_scope(tag + "_X1"):
            return pair_swap(value, "gx", 0)

    def link_pair(value, tag):
        with jax.named_scope(tag + "_X2"):
            return pair_swap(value, "gx", 1)

    def far(value, tag):
        with jax.named_scope(tag + "_far"):
            return pair_swap(value, "gy", 1)

    def near(value, tag):
        with jax.named_scope(tag + "_near"):
            return pair_swap(value, "gy", 0)

    def partners_of(value, tag):
        with jax.named_scope(tag + "_PT"):
            return [partner_swap(value, level) for level in range(1, levels + 1)]

    def other_side(value, partners, tag):
        if columns == 4:
            return core_pair(partners[0], tag + "_PT")
        return link_pair(value, tag)

    kv_far = far(own_kv, "kv")
    kv_near = near(own_kv, "kv")
    kv_pair = core_pair(own_kv, "kv")
    kv_partners = partners_of(after(own_kv, kv_pair), "kv")
    own_qd = jnp.stack([after(own_q, kv_pair), own_do])
    qd_pair = core_pair(after(own_qd, kv_pair), "qd")
    ready = after(kv_far, qd_pair)
    kv_far1, kv_far2 = core_pair(ready, "kvfar"), link_pair(ready, "kvfar")
    kv_other = other_side(own_kv, kv_partners, "kv")
    qd_partners = partners_of(after(own_qd, kv_partners), "qd")
    qd_far = far(after(own_qd, kv_far), "qd")
    qd_near = near(after(own_qd, kv_far), "qd")
    ready = after(kv_near, (kv_far1, kv_far2, kv_other))
    kv_near1, kv_near2 = core_pair(ready, "kvnear"), link_pair(ready, "kvnear")
    ready = after(qd_far, kv_near1)
    qd_far1, qd_far2 = core_pair(ready, "qdfar"), link_pair(ready, "qdfar")
    qd_other = other_side(own_qd, qd_partners, "qd")
    kv_blocks = [own_kv, kv_pair, kv_other] + kv_partners
    kv_blocks += [kv_far, kv_far1, kv_far2, kv_near, kv_near1, kv_near2]
    kv_blocks = [on_chip(block) for block in kv_blocks]

    shift_x = [0, side, -side] + [0] * levels + [0, side, -side] * 2
    shift_y = [0] * (3 + levels) + [-turn] * 3 + [turn] * 3
    count = len(kv_blocks)
    slots = [0] * (3 + levels) + [1] * 3 + [2] * 3
    shift_x = jnp.stack([jnp.asarray(v, jnp.int32) for v in shift_x])
    shift_y = jnp.stack([jnp.asarray(v, jnp.int32) for v in shift_y])
    position = jnp.arange(count)
    level = position - 2
    is_partner = (level >= 1) & (level <= levels)
    place = (shift_x + 1) * 3 + shift_y + 1
    flag = jnp.where(is_partner, 7 + level, jnp.where(place < 4, place, place - 1))
    mirrored = jnp.where(is_partner, 7 + level, 7 - flag)
    target_x = jnp.where(is_partner, column ^ (1 << jnp.maximum(level, 0)), column + shift_x)
    target_y = line + shift_y
    inside = (target_x >= 0) & (target_x < columns) & (target_y >= 0) & (target_y < lines)
    is_own = position == 0
    bits = pattern[0, 0]
    kinds = jnp.arange(bits.shape[0])
    chosen = jnp.sum(jnp.where(flag[:, None] == kinds[None], bits[None], 0), axis=1) > 0
    bias = jnp.where(is_own | (inside & chosen), 0.0, -PENALTY).astype(jnp.float32)
    index = jnp.clip(target_x, 0, columns - 1).astype(jnp.int32)
    lanes = jnp.arange(LANES)
    wanted = jnp.where(is_own, LANES - 1, jnp.where(inside, mirrored, -1))
    choose = (wanted[:, None] == lanes[None]).astype(jnp.float32)
    flags = jnp.pad((bits > 0).astype(jnp.float32), (0, LANES - bits.shape[0]))
    flags = jnp.where(lanes == LANES - 1, 1.0, flags)
    flags = jnp.broadcast_to(flags[None], (8, LANES))

    def call(kernel, inputs, outputs):
        return pl.pallas_call(
            kernel,
            out_shape=outputs,
            in_specs=[SMEM] + [VMEM] * (len(inputs) - 1),
            out_specs=jax.tree.map(lambda _: VMEM, outputs),
            compiler_params=PARAMS,
            cost_estimate=COST,
        )(*inputs)

    wide = jax.ShapeDtypeStruct((rows, width), jnp.bfloat16)
    table = jax.ShapeDtypeStruct((rows, LANES), jnp.float32)
    bias = after(bias, qd_far1)
    attended, columns_of, stats = call(
        functools.partial(attend_kernel, count),
        (bias, own_q, own_do, flags, *kv_blocks),
        (wide, table, jax.ShapeDtypeStruct((2 * heads + 8, LANES), jnp.float32)),
    )
    with jax.named_scope("stats_row"):
        row_stats = lax.all_gather(after(stats, (qd_near, qd_other)), "gx")
    ready = after(qd_near, row_stats)
    qd_near1, qd_near2 = core_pair(ready, "qdnear"), link_pair(ready, "qdnear")
    far_stats, near_stats = far(row_stats, "stats"), near(row_stats, "stats")
    query_grad = call(
        functools.partial(query_kernel, count),
        (bias, own_q, own_do, after(columns_of, row_stats), *kv_blocks),
        wide,
    )
    qd_blocks = [qd_pair, qd_other] + qd_partners
    qd_blocks += [qd_far, qd_far1, qd_far2, qd_near, qd_near1, qd_near2]
    qd_blocks = [on_chip(block) for block in qd_blocks]
    bases = [0] * len(qd_blocks)
    key_value_grad = pl.pallas_call(
        functools.partial(key_kernel, count, slots, bases),
        out_shape=jax.ShapeDtypeStruct(own_kv.shape, jnp.bfloat16),
        in_specs=[SMEM] + [VMEM] * (4 + count - 1 + 3),
        out_specs=VMEM,
        compiler_params=PARAMS,
        cost_estimate=COST,
    )(index, choose, own_kv, own_q, own_do, *qd_blocks, row_stats, far_stats, near_stats)
    return attended[None, None], query_grad[None, None], key_value_grad[None, None]


def solution(mesh):
    placed = (
        P("gx", "gy", None, None),
        P("gx", "gy", None, None, None),
        P("gx", "gy", None, None),
        P("gx", "gy", None),
    )
    return jax.shard_map(
        per_device,
        mesh=mesh,
        in_specs=placed,
        out_specs=(
            P("gx", "gy", None, None),
            P("gx", "gy", None, None),
            P("gx", "gy", None, None, None),
        ),
        check_vma=False,
    )
```

```python
import functools
import math

import jax
import jax.numpy as jnp
from jax import lax
from jax.experimental import pallas as pl
from jax.experimental.pallas import tpu as pltpu
from jax.sharding import PartitionSpec as P

E = 64
LANES = 128
PENALTY = 1e30
FOLD = math.log2(math.e) * float(E) ** (-0.5)
SCALE = float(E) ** (-0.5)
CONTRACT_LAST = (((1,), (1,)), ((), ()))


def pair_swap(value, axis, offset):
    pairs = []
    for first in range(offset, lax.axis_size(axis) - 1, 2):
        pairs += [(first, first + 1), (first + 1, first)]
    return lax.ppermute(value, axis, pairs)


def partner_swap(value, level):
    return lax.ppermute(value, "gx", [(i, i ^ (1 << level)) for i in range(lax.axis_size("gx"))])


def split_heads(block):
    low = lax.broadcasted_iota(jnp.int32, block.shape, 1) < E
    zero = jnp.zeros_like(block)
    return jnp.concatenate([jnp.where(low, block, zero), jnp.where(low, zero, block)], axis=0)


def join_heads(stacked):
    rows = stacked.shape[0] // 2
    low = lax.broadcasted_iota(jnp.int32, (rows, LANES), 1) < E
    return jnp.where(low, stacked[:rows], stacked[rows:])


def per_lane(columns, lane, first, table):
    rows = table.shape[0]
    table = jnp.where(lane == first, columns[:rows], table)
    return jnp.where(lane == first + 1, columns[rows:], table)


def from_lanes(table, first):
    return jnp.concatenate([table[:, first : first + 1], table[:, first + 1 : first + 2]], axis=0)


def masked_scores(q_ref, kv_refs, bias_ref, start, cols):
    rows = q_ref.shape[0]
    keys = jnp.concatenate([r[0, :, cols] for r in kv_refs], axis=0)
    scores = lax.dot_general(
        split_heads(q_ref[:, cols]), keys, CONTRACT_LAST, preferred_element_type=jnp.float32
    )
    return keys, [
        scores[:, b * rows : (b + 1) * rows] + bias_ref[start + b] for b in range(len(kv_refs))
    ]


def attend_kernel(count, bias_ref, q_ref, do_ref, flags_ref, *refs):
    kv_refs, (att_ref, columns_ref, stats_ref) = refs[:count], refs[count:]
    rows, width = q_ref.shape
    heads = width // E
    lane = lax.broadcasted_iota(jnp.int32, (rows, LANES), 1)
    low = lane < E
    columns = jnp.zeros((rows, LANES), jnp.float32)
    for pair in range(width // LANES):
        cols = slice(pair * LANES, (pair + 1) * LANES)
        values = jnp.concatenate([r[1, :, cols] for r in kv_refs], axis=0)
        _, scores = masked_scores(q_ref, kv_refs, bias_ref, 0, cols)
        scores = jnp.concatenate(scores, axis=1)
        largest = jnp.max(scores, axis=1, keepdims=True) * FOLD
        raised = jnp.exp2(scores * FOLD - largest)
        sums = jnp.dot(
            raised.astype(jnp.bfloat16),
            jnp.concatenate([values, jnp.ones_like(values)], axis=1),
            preferred_element_type=jnp.float32,
        )
        sums, totals = sums[:, :LANES], sums[:, LANES:]
        attended = join_heads(sums * (1.0 / totals)).astype(jnp.bfloat16)
        att_ref[:, cols] = attended
        product = do_ref[:, cols].astype(jnp.float32) * attended.astype(jnp.float32)
        delta = jnp.concatenate(
            [
                jnp.sum(jnp.where(low, product, 0.0), axis=1, keepdims=True),
                jnp.sum(jnp.where(low, 0.0, product), axis=1, keepdims=True),
            ],
            axis=0,
        )
        columns = per_lane(largest + jnp.log2(totals[:, :1]), lane, 2 * pair, columns)
        columns = per_lane(delta, lane, heads + 2 * pair, columns)
    columns_ref[...] = columns
    stats_ref[: 2 * heads] = columns.T[: 2 * heads]
    stats_ref[2 * heads :] = flags_ref[...]


def query_kernel(count, bias_ref, q_ref, do_ref, columns_ref, *refs):
    kv_refs, dq_ref = refs[:count], refs[count]
    rows, width = q_ref.shape
    heads = width // E
    columns = columns_ref[...]
    for pair in range(width // LANES):
        cols = slice(pair * LANES, (pair + 1) * LANES)
        values = jnp.concatenate([r[1, :, cols] for r in kv_refs], axis=0)
        keys, scores = masked_scores(q_ref, kv_refs, bias_ref, 0, cols)
        weights = jnp.exp2(
            jnp.concatenate(scores, axis=1) * FOLD - from_lanes(columns, 2 * pair)
        )
        prob_grad = lax.dot_general(
            split_heads(do_ref[:, cols]), values, CONTRACT_LAST, preferred_element_type=jnp.float32
        )
        delta = from_lanes(columns, heads + 2 * pair)
        score_grad = (weights * (prob_grad - delta)).astype(jnp.bfloat16)
        query_grad = jnp.dot(score_grad, keys, preferred_element_type=jnp.float32)
        dq_ref[:, cols] = (join_heads(query_grad) * SCALE).astype(jnp.bfloat16)


def key_kernel(count, slots, bases, index_ref, choose_ref, kv_ref, q_ref, do_ref, *refs):
    qd_refs = refs[: count - 1]
    stat_refs = refs[count - 1 : count + 2]
    out_ref = refs[count + 2]
    rows, width = q_ref.shape
    heads = width // E
    levels, deltas = [], []
    for b in range(count):
        stat = stat_refs[slots[b]][index_ref[b]]
        flag = jnp.sum(
            stat[2 * heads : 2 * heads + 1] * choose_ref[b : b + 1], axis=1, keepdims=True
        )
        levels.append(stat[:heads] + jnp.where(flag > 0.5, 0.0, PENALTY))
        deltas.append(stat[heads : 2 * heads])
    levels = jnp.concatenate(levels, axis=1)
    deltas = jnp.concatenate(deltas, axis=1)

    def per_head(table, pair):
        shape = (rows, table.shape[1])
        return jnp.concatenate(
            [jnp.broadcast_to(table[2 * pair + h : 2 * pair + h + 1], shape) for h in range(2)],
            axis=0,
        )

    for pair in range(width // LANES):
        cols = slice(pair * LANES, (pair + 1) * LANES)
        queries = jnp.concatenate([q_ref[:, cols]] + [r[o, :, cols] for r, o in zip(qd_refs, bases)], axis=0)
        grads = jnp.concatenate([do_ref[:, cols]] + [r[o + 1, :, cols] for r, o in zip(qd_refs, bases)], axis=0)
        scores = lax.dot_general(
            split_heads(kv_ref[0, :, cols]),
            queries,
            CONTRACT_LAST,
            preferred_element_type=jnp.float32,
        )
        weights = jnp.exp2(scores * FOLD - per_head(levels, pair))
        value_grad = jnp.dot(
            weights.astype(jnp.bfloat16), grads, preferred_element_type=jnp.float32
        )
        prob_grad = lax.dot_general(
            split_heads(kv_ref[1, :, cols]),
            grads,
            CONTRACT_LAST,
            preferred_element_type=jnp.float32,
        )
        score_grad = (weights * (prob_grad - per_head(deltas, pair))).astype(jnp.bfloat16)
        key_grad = jnp.dot(score_grad, queries, preferred_element_type=jnp.float32)
        out_ref[0, :, cols] = (join_heads(key_grad) * SCALE).astype(jnp.bfloat16)
        out_ref[1, :, cols] = join_heads(value_grad).astype(jnp.bfloat16)


def after(value, other):
    return lax.optimization_barrier((value, other))[0]


def both(a, b):
    return lax.optimization_barrier((a, b))


def on_chip(value):
    return pltpu.with_memory_space_constraint(value, pltpu.MemorySpace.VMEM)


PARAMS = pltpu.CompilerParams(vmem_limit_bytes=14 * 2**20)
VMEM = pl.BlockSpec(memory_space=pltpu.VMEM)
SMEM = pl.BlockSpec(memory_space=pltpu.SMEM)


COST = pl.CostEstimate(flops=128, bytes_accessed=128, transcendentals=0)


def per_device(queries, keys_values, out_grad, pattern):
    own_q, own_kv, own_do = queries[0, 0], keys_values[0, 0], out_grad[0, 0]
    rows, width = own_q.shape
    heads = width // E
    columns, lines = lax.axis_size("gx"), lax.axis_size("gy")
    levels = columns.bit_length() - 2
    column, line = lax.axis_index("gx"), lax.axis_index("gy")
    side = 1 - 2 * (column % 2)
    turn = 1 - 2 * (line % 2)

    def core_pair(value, tag):
        with jax.named_scope(tag + "_X1"):
            return pair_swap(value, "gx", 0)

    def link_pair(value, tag):
        with jax.named_scope(tag + "_X2"):
            return pair_swap(value, "gx", 1)

    def far(value, tag):
        with jax.named_scope(tag + "_far"):
            return pair_swap(value, "gy", 1)

    def near(value, tag):
        with jax.named_scope(tag + "_near"):
            return pair_swap(value, "gy", 0)

    def partners_of(value, tag):
        with jax.named_scope(tag + "_PT"):
            return [partner_swap(value, level) for level in range(1, levels + 1)]

    def other_side(value, partners, tag):
        if columns == 4:
            return core_pair(partners[0], tag + "_PT")
        return link_pair(value, tag)

    kv_far = far(own_kv, "kv")
    kv_near = near(own_kv, "kv")
    kv_pair = core_pair(own_kv, "kv")
    kv_partners = partners_of(after(own_kv, kv_pair), "kv")
    own_qd = jnp.stack([after(own_q, kv_pair), own_do])
    qd_pair = core_pair(after(own_qd, kv_pair), "qd")
    ready = after(kv_far, qd_pair)
    kv_far1, kv_far2 = core_pair(ready, "kvfar"), link_pair(ready, "kvfar")
    kv_other = other_side(own_kv, kv_partners, "kv")
    qd_partners = partners_of(after(own_qd, kv_partners), "qd")
    qd_far = far(after(own_qd, kv_far), "qd")
    qd_near = near(after(own_qd, kv_far), "qd")
    ready = after(kv_near, (kv_far1, kv_far2, kv_other))
    kv_near1, kv_near2 = core_pair(ready, "kvnear"), link_pair(ready, "kvnear")
    ready = after(qd_far, kv_near1)
    qd_far1, qd_far2 = core_pair(ready, "qdfar"), link_pair(ready, "qdfar")
    qd_other = other_side(own_qd, qd_partners, "qd")
    kv_blocks = [own_kv, kv_pair, kv_other] + kv_partners
    kv_blocks += [kv_far, kv_far1, kv_far2, kv_near, kv_near1, kv_near2]
    kv_blocks = [on_chip(block) for block in kv_blocks]

    shift_x = [0, side, -side] + [0] * levels + [0, side, -side] * 2
    shift_y = [0] * (3 + levels) + [-turn] * 3 + [turn] * 3
    count = len(kv_blocks)
    slots = [0] * (3 + levels) + [1] * 3 + [2] * 3
    shift_x = jnp.stack([jnp.asarray(v, jnp.int32) for v in shift_x])
    shift_y = jnp.stack([jnp.asarray(v, jnp.int32) for v in shift_y])
    position = jnp.arange(count)
    level = position - 2
    is_partner = (level >= 1) & (level <= levels)
    place = (shift_x + 1) * 3 + shift_y + 1
    flag = jnp.where(is_partner, 7 + level, jnp.where(place < 4, place, place - 1))
    mirrored = jnp.where(is_partner, 7 + level, 7 - flag)
    target_x = jnp.where(is_partner, column ^ (1 << jnp.maximum(level, 0)), column + shift_x)
    target_y = line + shift_y
    inside = (target_x >= 0) & (target_x < columns) & (target_y >= 0) & (target_y < lines)
    is_own = position == 0
    bits = pattern[0, 0]
    kinds = jnp.arange(bits.shape[0])
    chosen = jnp.sum(jnp.where(flag[:, None] == kinds[None], bits[None], 0), axis=1) > 0
    bias = jnp.where(is_own | (inside & chosen), 0.0, -PENALTY).astype(jnp.float32)
    index = jnp.clip(target_x, 0, columns - 1).astype(jnp.int32)
    lanes = jnp.arange(LANES)
    wanted = jnp.where(is_own, LANES - 1, jnp.where(inside, mirrored, -1))
    choose = (wanted[:, None] == lanes[None]).astype(jnp.float32)
    flags = jnp.pad((bits > 0).astype(jnp.float32), (0, LANES - bits.shape[0]))
    flags = jnp.where(lanes == LANES - 1, 1.0, flags)
    flags = jnp.broadcast_to(flags[None], (8, LANES))

    def call(kernel, inputs, outputs):
        return pl.pallas_call(
            kernel,
            out_shape=outputs,
            in_specs=[SMEM] + [VMEM] * (len(inputs) - 1),
            out_specs=jax.tree.map(lambda _: VMEM, outputs),
            compiler_params=PARAMS,
            cost_estimate=COST,
        )(*inputs)

    wide = jax.ShapeDtypeStruct((rows, width), jnp.bfloat16)
    table = jax.ShapeDtypeStruct((rows, LANES), jnp.float32)
    near_q, near_do = on_chip(own_q), on_chip(own_do)
    bias = after(bias, qd_far1)
    attended, columns_of, stats = call(
        functools.partial(attend_kernel, count),
        (bias, near_q, near_do, on_chip(flags), *kv_blocks),
        (wide, table, jax.ShapeDtypeStruct((2 * heads + 8, LANES), jnp.float32)),
    )
    with jax.named_scope("stats_row"):
        row_stats = lax.all_gather(after(stats, qd_other), "gx")
    ready = after(qd_near, row_stats)
    qd_near1, qd_near2 = core_pair(ready, "qdnear"), link_pair(ready, "qdnear")
    far_stats, near_stats = far(row_stats, "stats"), near(row_stats, "stats")
    query_grad = call(
        functools.partial(query_kernel, count),
        (bias, near_q, near_do, on_chip(after(columns_of, row_stats)), *kv_blocks),
        wide,
    )
    qd_blocks = [qd_pair, qd_other] + qd_partners
    qd_blocks += [qd_far, qd_far1, qd_far2, qd_near, qd_near1, qd_near2]
    qd_blocks = [on_chip(block) for block in qd_blocks]
    bases = [0] * len(qd_blocks)
    key_value_grad = pl.pallas_call(
        functools.partial(key_kernel, count, slots, bases),
        out_shape=jax.ShapeDtypeStruct(own_kv.shape, jnp.bfloat16),
        in_specs=[SMEM] + [VMEM] * (4 + count - 1 + 3),
        out_specs=VMEM,
        compiler_params=PARAMS,
        cost_estimate=COST,
    )(
        index,
        on_chip(choose),
        kv_blocks[0],
        near_q,
        near_do,
        *qd_blocks,
        *[on_chip(v) for v in (row_stats, far_stats, near_stats)],
    )
    return attended[None, None], query_grad[None, None], key_value_grad[None, None]


def solution(mesh):
    placed = (
        P("gx", "gy", None, None),
        P("gx", "gy", None, None, None),
        P("gx", "gy", None, None),
        P("gx", "gy", None),
    )
    return jax.shard_map(
        per_device,
        mesh=mesh,
        in_specs=placed,
        out_specs=(
            P("gx", "gy", None, None),
            P("gx", "gy", None, None),
            P("gx", "gy", None, None, None),
        ),
        check_vma=False,
    )
```
